1024 devices in a mesh: ctx: 128 (over z_lo, y, x), head: 8 (over z_hi, core).
Axes of the slice: x: 4, y: 4, z: 32 (z_hi: 4, z_lo: 8; z = z_hi * 8 + z_lo), core: 2. Of those that a mesh axis runs over, the one named last changes fastest.
Arguments:
- queries: bfloat16 [32768, 8192], P('ctx', 'head'), may hold values from -120 to 120, as said below
- keys: bfloat16 [32768, 1024], P(('ctx', 'head')), may hold values from -6 to 6
- values: bfloat16 [32768, 1024], P(('ctx', 'head')), may hold values from -6 to 6
- doc_ids: int32 [32768], replicated, may hold values from 0 to 255, never falling along the last dimension, each value on 1 to 512 neighbouring positions
- output_gradient: bfloat16 [32768, 8192], P('ctx', 'head'), may hold values from -6 to 6
Outputs:
- attended: bfloat16 [32768, 8192], P('ctx', 'head')
- query_grad: bfloat16 [32768, 8192], P('ctx', 'head')
- key_grad: bfloat16 [32768, 1024], P(('ctx', 'head'))
- value_grad: bfloat16 [32768, 1024], P(('ctx', 'head'))
The draws below stay inside these ranges and needn't reach their ends.
Inputs may be any that keep to these rules, and one draw needn't show every extreme that they name: `queries`: queries lie within -120 to 120 (up to 20 times a key entry), so scores may exceed 200.
All inputs are finite; a program needn't handle non-finite values.
Results may differ from the reference program's by a relative error of at most 0.012.
The reference program's roundings to bfloat16 on the way (of `weights` and `score_grad`) count: a program that leaves them out, or rounds other values in their place, can miss the bound.
Values may be sent and summed in bfloat16 or wider, within the bound.
A program may use at most 32 MiB of HBM per device.

```python
import math
import jax
import jax.numpy as jnp
import numpy as np
from jax import lax

QUERY_HEADS = 64
KEY_VALUE_HEADS = 8
HEAD_SIZE = 128
TOK_DEV = 256
SPAN = 2
PACKED_TOKENS = 32768
DOC_MAX = 512
DOCS = 256
N_CTX = 128


def query_key_pair(key):
    query_group_width = QUERY_HEADS // KEY_VALUE_HEADS
    random_key_seed = jax.random.fold_in(key, 11)
    random_query_seed = jax.random.fold_in(key, 12)
    sampled_keys = jax.random.truncated_normal(random_key_seed, -6.0, 6.0, (PACKED_TOKENS, KEY_VALUE_HEADS, HEAD_SIZE), jnp.float32)
    sampled_queries = jax.random.truncated_normal(random_query_seed, -6.0, 6.0, (PACKED_TOKENS, KEY_VALUE_HEADS, query_group_width, HEAD_SIZE), jnp.float32)
    return (sampled_queries.reshape(PACKED_TOKENS, QUERY_HEADS * HEAD_SIZE), sampled_keys.reshape(PACKED_TOKENS, KEY_VALUE_HEADS * HEAD_SIZE))


def draw_queries(key, part):
    return query_key_pair(key)[0].astype(jnp.bfloat16)


def draw_keys(key, part):
    return query_key_pair(key)[1].astype(jnp.bfloat16)


def block_scale(stream_key, extent, cuts, least, high):
    def one(axis_at, parts):
        heights = jax.random.uniform(jax.random.fold_in(jax.random.fold_in(stream_key, 6), axis_at), (parts,), jnp.float32, least / len(cuts), high / len(cuts))
        return jnp.repeat(jnp.exp(heights), extent[axis_at] // parts).reshape((-1,) + (1,) * (len(extent) - axis_at - 1))

    loudness = one(*cuts[0])
    for cut in cuts[1:]:
        loudness = loudness * one(*cut)
    return loudness


def length_profile(amount, total, most, slope):
    loads = [(1 << 20) // math.isqrt(grade ** slope) + 1 for grade in range(2, amount + 1)]
    rest, holding = total - most - (amount - 1), [1] * (amount - 1)
    while rest > 0:
        candidates = [i for i in range(amount - 1) if holding[i] < most]
        mass, left = sum([loads[i] for i in candidates]), rest
        for i in candidates:
            addition = min(most - holding[i], max(1, left * loads[i] // mass), rest)
            holding[i] = holding[i] + addition
            rest = rest - addition
    return np.array([most] + holding)


def ragged(key, number_of, total, bound, slope):
    if number_of == 2:
        one = jax.random.randint(key, (), max(1, total - bound), min(bound, total - 1) + 1)
        return jnp.stack([one, total - one])
    tallies = jnp.asarray(length_profile(number_of, total, bound, slope), jnp.int32)
    twos = (number_of - 1) // 2
    donor, taker = tallies[1:1 + 2 * twos:2], tallies[2:2 + 2 * twos:2]
    margin = jnp.minimum(donor - 1, bound - taker)
    shifted = jax.random.randint(jax.random.fold_in(key, 1), (twos,), 0, 1 << 20) % (margin + 1)
    tallies = tallies.at[1:1 + 2 * twos:2].set(donor - shifted).at[2:2 + 2 * twos:2].set(taker + shifted)
    return tallies[jax.random.permutation(jax.random.fold_in(key, 2), number_of)]


def scatter_about(stream_key, shape, spread, most, split=(), kind=jnp.bfloat16):
    drawn = spread * jax.random.normal(stream_key, shape, jnp.float32)
    if split:
        drawn = drawn * block_scale(stream_key, shape, split, -0.22, 0.18)
    return jnp.clip(drawn, -most, most).astype(kind)


def setup_inputs(seed: int = 0) -> dict:
    key_of = jax.random.split(jax.random.key(seed), 6)
    return {
        "queries": draw_queries(jax.random.fold_in(key_of[5], 71), 0),
        "keys": draw_keys(jax.random.fold_in(key_of[5], 71), 0),
        "values": scatter_about(key_of[2], (PACKED_TOKENS, KEY_VALUE_HEADS * HEAD_SIZE), 1.0, 6.0, ((0, 1024),)),
        "doc_ids": jnp.searchsorted(jnp.cumsum(ragged(key_of[3], DOCS, PACKED_TOKENS, DOC_MAX, 2)), jnp.arange(PACKED_TOKENS), side="right").astype(jnp.int32),
        "output_gradient": scatter_about(key_of[4], (PACKED_TOKENS, QUERY_HEADS * HEAD_SIZE), 1.0, 6.0, ((0, 128), (1, 8))),
    }


masked_value = -1.0e30


def doc_visible(doc_ids, query_start, key_start, query_count, key_count, margin_rows):
    padded = jnp.concatenate([jnp.full((margin_rows,), -1, jnp.int32), doc_ids.astype(jnp.int32), jnp.full((margin_rows,), -2, jnp.int32)])
    query_docs = lax.dynamic_slice_in_dim(padded, (query_start + margin_rows).astype(jnp.int32), query_count, 0)
    key_docs = lax.dynamic_slice_in_dim(padded, (key_start + margin_rows).astype(jnp.int32), key_count, 0)
    query_places = query_start + jnp.arange(query_count, dtype=jnp.int32)
    key_places = key_start + jnp.arange(key_count, dtype=jnp.int32)
    return (key_places[None, :] <= query_places[:, None]) & (key_docs[None, :] == query_docs[:, None])


def reference(queries, keys, values, doc_ids, output_gradient):
    row_total = TOK_DEV
    margin_rows = SPAN * row_total
    visible_span = margin_rows + row_total
    query_group_width = QUERY_HEADS // KEY_VALUE_HEADS
    key_value_width = KEY_VALUE_HEADS * HEAD_SIZE
    score_scale = HEAD_SIZE ** -0.5
    high = lax.Precision.HIGHEST
    padding_keys = jnp.concatenate([jnp.zeros((margin_rows, key_value_width), keys.dtype), keys], 0)
    padding_values = jnp.concatenate([jnp.zeros((margin_rows, key_value_width), values.dtype), values], 0)

    def shard_step(carry, shard_index):
        key_acc, value_acc = carry
        offset_position = (shard_index * row_total).astype(jnp.int32)
        query_row_block = lax.dynamic_slice_in_dim(queries, offset_position, row_total, 0).astype(jnp.float32).reshape(row_total, KEY_VALUE_HEADS, query_group_width, HEAD_SIZE)
        gradient_row_block = lax.dynamic_slice_in_dim(output_gradient, offset_position, row_total, 0).astype(jnp.float32).reshape(row_total, KEY_VALUE_HEADS, query_group_width, HEAD_SIZE)
        key_row_block = lax.dynamic_slice_in_dim(padding_keys, offset_position, visible_span, 0).astype(jnp.float32).reshape(visible_span, KEY_VALUE_HEADS, HEAD_SIZE)
        value_row_block = lax.dynamic_slice_in_dim(padding_values, offset_position, visible_span, 0).astype(jnp.float32).reshape(visible_span, KEY_VALUE_HEADS, HEAD_SIZE)
        visible = doc_visible(doc_ids, offset_position, offset_position - margin_rows, row_total, visible_span, margin_rows)
        scores = jnp.einsum("tkgd,wkd->kgtw", query_row_block, key_row_block, precision=high) * score_scale
        scores = jnp.where(visible[None, None], scores, masked_value)
        row_max = jnp.max(scores, axis=3, keepdims=True)
        row_sum = jnp.sum(jnp.exp(scores - row_max), axis=3, keepdims=True)
        log_totals = row_max + jnp.log(row_sum)
        probabilities = jnp.where(visible[None, None], jnp.exp(scores - log_totals), 0.0)
        weights = probabilities.astype(jnp.bfloat16).astype(jnp.float32)
        attended = jnp.einsum("kgtw,wkd->tkgd", weights, value_row_block, precision=high).astype(jnp.bfloat16)
        deltas = jnp.einsum("tkgd,tkgd->kgt", gradient_row_block, attended.astype(jnp.float32), precision=high)
        prob_grad = jnp.einsum("tkgd,wkd->kgtw", gradient_row_block, value_row_block, precision=high)
        score_grad = (probabilities * (prob_grad - deltas[..., None]) * score_scale).astype(jnp.bfloat16)
        score_grad = lax.optimization_barrier(score_grad).astype(jnp.float32)
        query_grad = jnp.einsum("kgtw,wkd->tkgd", score_grad, key_row_block, precision=high).astype(jnp.bfloat16)
        key_part = jnp.einsum("kgtw,tkgd->wkd", score_grad, query_row_block, precision=high).reshape(visible_span, key_value_width)
        value_part = jnp.einsum("kgtw,tkgd->wkd", weights, gradient_row_block, precision=high).reshape(visible_span, key_value_width)
        old_keys = lax.dynamic_slice_in_dim(key_acc, offset_position, visible_span, 0)
        old_values = lax.dynamic_slice_in_dim(value_acc, offset_position, visible_span, 0)
        key_acc = lax.dynamic_update_slice_in_dim(key_acc, old_keys + key_part, offset_position, 0)
        value_acc = lax.dynamic_update_slice_in_dim(value_acc, old_values + value_part, offset_position, 0)
        return (key_acc, value_acc), (attended.reshape(row_total, QUERY_HEADS * HEAD_SIZE), query_grad.reshape(row_total, QUERY_HEADS * HEAD_SIZE))

    zeros_acc = jnp.zeros((margin_rows + PACKED_TOKENS, key_value_width), jnp.float32)
    (key_acc, value_acc), (attended_all, query_all) = lax.scan(shard_step, (zeros_acc, zeros_acc), jnp.arange(N_CTX, dtype=jnp.int32))
    attended_all = attended_all.reshape(PACKED_TOKENS, QUERY_HEADS * HEAD_SIZE)
    query_all = query_all.reshape(PACKED_TOKENS, QUERY_HEADS * HEAD_SIZE)
    return attended_all, query_all, key_acc[margin_rows:].astype(jnp.bfloat16), value_acc[margin_rows:].astype(jnp.bfloat16)
```

```python
import functools
import math

import jax
import jax.numpy as jnp
from jax import lax
from jax.experimental import pallas as pl
from jax.experimental.pallas import tpu as pltpu
from jax.sharding import PartitionSpec as P

HEAD_SIZE = 128
TILE = 128
SPAN = 2
GROUPS = 4
SCALE = HEAD_SIZE ** -0.5
EXP2_SCALE = SCALE * math.log2(math.e)
MASKED = -1e30
MESH = pl.DeviceIdType.MESH
F32 = jnp.float32
BF16 = jnp.bfloat16


def dot_nt(a, b):
    return lax.dot_general(a, b, (((1,), (1,)), ((), ())), preferred_element_type=F32)


def dot_nn(a, b):
    return lax.dot_general(a, b, (((1,), (0,)), ((), ())), preferred_element_type=F32)


def kernel(
    n_ctx,
    q_hbm,
    k_hbm,
    v_hbm,
    doc_hbm,
    g_hbm,
    att_hbm,
    dq_hbm,
    dk_hbm,
    dv_hbm,
    stage,
    window,
    relay,
    doc,
    qs,
    gs,
    qt,
    gt,
    bias,
    probs,
    weights,
    score_grad,
    att_out,
    dq_out,
    acc,
    part,
    own,
    got,
    home,
    back_relay,
    result,
    load_sem,
    head_load_sem,
    self_sem,
    out_sem,
    result_sem,
    fwd_send,
    fwd_recv,
    fwd_relay_recv,
    ctx_send,
    ctx_recv,
    back_ctx_send,
    back_ctx_recv,
    back_send,
    back_recv,
    back_relay_recv,
):
    rows = TILE * 2
    piece = stage.shape[1]
    group_rows = 2 * piece
    heads = qs.shape[1] // TILE
    reach = SPAN * rows + TILE
    ctx = lax.axis_index("ctx")
    head = lax.axis_index("head")
    zone = head // 2
    core = lax.rem(head, 2)

    def zone_at(offset):
        return lax.rem(zone + offset, GROUPS)

    far, plus, minus = zone_at(2), zone_at(1), zone_at(3)
    relative = (far, plus, minus, zone)
    partner = zone * 2 + (1 - core)

    has_later = (ctx + 1 < n_ctx, ctx + 2 < n_ctx)
    has_earlier = (ctx >= 1, ctx >= 2)

    barrier = pltpu.get_barrier_semaphore()
    for peer in (plus * 2, plus * 2 + 1, minus * 2, minus * 2 + 1, partner):
        pl.semaphore_signal(barrier, inc=1, device_id=(ctx, peer), device_id_type=MESH)
    for dist in (1, 2):

        @pl.when(has_later[dist - 1])
        def _():
            pl.semaphore_signal(
                barrier, inc=1, device_id=(ctx + dist, head), device_id_type=MESH
            )

        @pl.when(has_earlier[dist - 1])
        def _():
            pl.semaphore_signal(
                barrier, inc=1, device_id=(ctx - dist, head), device_id_type=MESH
            )

    loads = [
        pltpu.make_async_copy(k_hbm, stage.at[0], load_sem.at[0]),
        pltpu.make_async_copy(v_hbm, stage.at[1], load_sem.at[1]),
        pltpu.make_async_copy(doc_hbm, doc, load_sem.at[2]),
    ]
    for copy in loads:
        copy.start()
    head_loads = []
    for which, (source, target) in enumerate(((q_hbm, qs), (g_hbm, gs))):
        for i in range(2):
            for h in range(heads):
                copy = pltpu.make_async_copy(
                    source.at[pl.ds(i * TILE, TILE), pl.ds(h * TILE, TILE)],
                    target.at[i, pl.ds(h * TILE, TILE), :],
                    head_load_sem.at[which, i, h],
                )
                copy.start()
                head_loads.append(copy)

    zero_block = jnp.zeros((rows, HEAD_SIZE), BF16)

    @pl.when(ctx < 1)
    def _():
        for a in range(2):
            window[a, pl.ds(rows, rows), :] = zero_block

    @pl.when(ctx < 2)
    def _():
        for a in range(2):
            window[a, pl.ds(0, rows), :] = zero_block

    for dist in (1, 2):

        @pl.when(ctx + dist >= n_ctx)
        def _():
            for a in range(2):
                got[a, dist - 1] = zero_block

    acc[...] = jnp.zeros_like(acc)

    def columns(of_head):
        return pl.ds(pl.multiple_of(of_head * HEAD_SIZE, HEAD_SIZE), HEAD_SIZE)

    def piece_rows(of_head, base=0):
        return pl.ds(pl.multiple_of(base + of_head * piece, piece), piece)

    def zone_rows(of_zone, base=0):
        return pl.ds(pl.multiple_of(base + of_zone * group_rows, group_rows), group_rows)

    loads[0].wait()
    loads[1].wait()
    self_copies = []
    for a in range(2):
        copy = pltpu.make_async_copy(
            stage.at[a, :, columns(head)],
            window.at[a, piece_rows(head, SPAN * rows), :],
            self_sem.at[a],
        )
        copy.start()
        self_copies.append(copy)
    loads[2].wait()

    row_place = lax.broadcasted_iota(jnp.int32, (TILE, TILE), 0)
    column_place = lax.broadcasted_iota(jnp.int32, (TILE, TILE), 1)
    for i in range(2):
        query_docs = jnp.broadcast_to(
            doc[pl.ds(2 * ctx + i, 1), :].astype(F32), (TILE, TILE)
        ).T
        for j in range(5):
            doc_row = 2 * ctx - 2 * SPAN + i + j
            key_docs = doc[pl.ds(jnp.maximum(doc_row, 0), 1), :].astype(F32)
            seen = query_docs == key_docs
            if j == 4:
                seen = seen & (column_place <= row_place)
            outside = jnp.where(doc_row >= 0, 0.0, MASKED).astype(F32)
            bias[i, :, pl.ds(j * TILE, TILE)] = jnp.where(seen, 0.0, MASKED) + outside

    for copy in head_loads:
        copy.wait()
    for i in range(2):
        for h in range(heads):
            at = pl.ds(h * TILE, TILE)
            qt[i, :, at] = qs[i, at, :].T
            gt[i, :, at] = gs[i, at, :].T

    pl.semaphore_wait(
        barrier,
        5
        + has_later[0].astype(jnp.int32)
        + has_later[1].astype(jnp.int32)
        + has_earlier[0].astype(jnp.int32)
        + has_earlier[1].astype(jnp.int32),
    )

    sends = []

    def remote(source, target, send_sem, recv_sem, device):
        return pltpu.make_async_remote_copy(
            src_ref=source,
            dst_ref=target,
            send_sem=send_sem,
            recv_sem=recv_sem,
            device_id=device,
            device_id_type=MESH,
        )

    def send(source, target, send_sem, recv_sem, device):
        copy = remote(source, target, send_sem, recv_sem, device)
        copy.start()
        sends.append((copy, None))

    def send_if(wanted, source, target, send_sem, recv_sem, device):
        copy = remote(source, target, send_sem, recv_sem, device)

        @pl.when(wanted)
        def _():
            copy.start()

        sends.append((copy, wanted))

    def arrived(target, recv_sem):
        remote(target, target, fwd_send.at[0, 0], recv_sem, (ctx, partner)).wait_recv()

    def exchange_far(source_of, relay_ref, send_sem, recv_sem):
        for way, (middle, target_core) in enumerate(((plus, core), (minus, 1 - core))):
            send(
                source_of(far * 2 + target_core),
                relay_ref.at[way],
                send_sem.at[way],
                recv_sem.at[way],
                (ctx, middle * 2 + target_core),
            )

    def exchange_near(source_of, target, zone_number, send_sem, recv_sem, slot):
        for target_core in range(2):
            peer = zone_number * 2 + target_core
            send(source_of(peer), target, send_sem.at[slot + target_core], recv_sem, (ctx, peer))

    def pass_on(relay_ref, target_of, send_sem, relay_recv, recv_of):
        for way, (after, origin) in enumerate(
            ((plus, minus * 2 + core), (minus, plus * 2 + (1 - core)))
        ):
            arrived(relay_ref.at[way], relay_recv.at[way])
            send(
                relay_ref.at[way],
                target_of(origin),
                send_sem.at[7 + way],
                recv_of(origin),
                (ctx, after * 2 + core),
            )

    for a in range(2):
        source_of = lambda to_head: stage.at[a, :, columns(to_head)]
        mine = window.at[a, piece_rows(head, SPAN * rows), :]
        exchange_far(source_of, relay.at[a], fwd_send.at[a], fwd_relay_recv.at[a])
        exchange_near(source_of, mine, plus, fwd_send.at[a], fwd_recv.at[a, head], 2)
        exchange_near(source_of, mine, minus, fwd_send.at[a], fwd_recv.at[a, head], 4)
        send(
            source_of(partner), mine, fwd_send.at[a, 6], fwd_recv.at[a, head], (ctx, partner)
        )

    def window_piece(a, of_head):
        return window.at[a, piece_rows(of_head, SPAN * rows), :]

    def hand_on(a, r):
        group = relative[r]
        if r == 3:
            self_copies[a].wait()
            arrived(window_piece(a, partner), fwd_recv.at[a, partner])
        else:
            for source_core in range(2):
                origin = group * 2 + source_core
                arrived(window_piece(a, origin), fwd_recv.at[a, origin])
        for dist in (1, 2):
            send_if(
                has_later[dist - 1],
                window.at[a, zone_rows(group, SPAN * rows), :],
                window.at[a, zone_rows(group, (SPAN - dist) * rows), :],
                ctx_send.at[a, dist - 1, r],
                ctx_recv.at[a, dist - 1, r],
                (ctx + dist, head),
            )

    def relay_forward(a):
        pass_on(
            relay.at[a],
            lambda origin: window_piece(a, origin),
            fwd_send.at[a],
            fwd_relay_recv.at[a],
            lambda origin: fwd_recv.at[a, origin],
        )

    hand_on(0, 3)
    hand_on(1, 3)
    relay_forward(0)
    hand_on(0, 1)
    hand_on(0, 2)
    relay_forward(1)
    hand_on(1, 1)
    hand_on(1, 2)
    hand_on(0, 0)
    hand_on(1, 0)

    def window_here(a):
        for r in (3, 1, 2, 0):
            for dist in (1, 2):

                @pl.when(has_earlier[dist - 1])
                def _():
                    arrived(
                        window.at[a, zone_rows(relative[r], (SPAN - dist) * rows), :],
                        ctx_recv.at[a, dist - 1, r],
                    )

    blocks = heads // 2

    def block_of(n):
        i = n // blocks
        at = pl.ds(pl.multiple_of(lax.rem(n, blocks) * (2 * TILE), 2 * TILE), 2 * TILE)
        span = pl.ds(pl.multiple_of(i * TILE, TILE), reach)
        return i, at, span

    window_here(0)

    def probability_step(n, carry):
        i, at, span = block_of(n)
        scores = dot_nt(qs[i, at, :], window[0, span, :])
        mask = bias[i]
        scores = scores + jnp.concatenate([mask, mask], 0)
        row_max = jnp.max(scores, axis=1, keepdims=True)
        raised = jnp.exp2((scores - row_max) * EXP2_SCALE)
        inverse = 1.0 / jnp.sum(raised, axis=1, keepdims=True)
        probability = raised * inverse
        probs[i, at, :] = probability
        weights[i, at, :] = probability.astype(BF16)
        return carry

    lax.fori_loop(0, 2 * blocks, probability_step, 0)

    def collect(g, left, right):
        for i in range(2):
            span = pl.ds(i * TILE, reach)
            acc[g, :, span] = acc[g, :, span] + dot_nn(left[i], right[i])
        for t in range(2 * SPAN + 2):
            block = acc[g, :, pl.ds(t * TILE, TILE)].T
            if t < 2 * SPAN:
                part[g, pl.ds(t * TILE, TILE), :] = block.astype(BF16)
            else:
                own[g, pl.ds(t * TILE - SPAN * rows, TILE), :] = block
        for r in range(GROUPS):
            for dist in (1, 2):
                send_if(
                    has_earlier[dist - 1],
                    part.at[g, zone_rows(relative[r], (SPAN - dist) * rows), :],
                    got.at[g, dist - 1, zone_rows(relative[r]), :],
                    back_ctx_send.at[g, dist - 1, r],
                    back_ctx_recv.at[g, dist - 1, r],
                    (ctx - dist, head),
                )

    collect(1, gt, weights)

    window_here(1)

    def gradient_step(n, carry):
        i, at, span = block_of(n)
        value_window = window[1, span, :]
        out_gradient = gs[i, at, :]
        attended = dot_nn(weights[i, at, :], value_window).astype(BF16)
        att_out[i, at, :] = attended
        delta = jnp.sum(
            out_gradient.astype(F32) * attended.astype(F32), axis=1, keepdims=True
        )
        prob_grad = dot_nt(out_gradient, value_window)
        score_grad[i, at, :] = (probs[i, at, :] * (prob_grad - delta) * SCALE).astype(BF16)
        return carry

    lax.fori_loop(0, 2 * blocks, gradient_step, 0)
    collect(0, qt, score_grad)

    outs = []

    def write_out(which, source, target):
        for i in range(2):
            for h in range(heads):
                copy = pltpu.make_async_copy(
                    source.at[i, pl.ds(h * TILE, TILE), :],
                    target.at[pl.ds(i * TILE, TILE), pl.ds(h * TILE, TILE)],
                    out_sem.at[which, i, h],
                )
                copy.start()
                outs.append(copy)

    write_out(0, att_out, att_hbm)

    self_results = []

    def send_home(g):
        mine = result.at[g, :, columns(head)]
        source_of = lambda to_head: home.at[g, piece_rows(to_head), :]
        for r in range(GROUPS):
            at = zone_rows(relative[r])
            for dist in (1, 2):

                @pl.when(has_later[dist - 1])
                def _():
                    arrived(got.at[g, dist - 1, at, :], back_ctx_recv.at[g, dist - 1, r])

            total = own[g, at, :] + got[g, 0, at, :].astype(F32) + got[g, 1, at, :].astype(F32)
            home[g, at, :] = total.astype(BF16)
            if r == 0:
                exchange_far(source_of, back_relay.at[g], back_send.at[g], back_relay_recv.at[g])
            elif r < 3:
                exchange_near(
                    source_of, mine, relative[r], back_send.at[g], back_recv.at[g, head], 2 * r
                )
            else:
                send(
                    source_of(partner),
                    mine,
                    back_send.at[g, 6],
                    back_recv.at[g, head],
                    (ctx, partner),
                )
                copy = pltpu.make_async_copy(source_of(head), mine, self_sem.at[2 + g])
                copy.start()
                self_results.append(copy)

    def relay_home(g):
        pass_on(
            back_relay.at[g],
            lambda origin: result.at[g, :, columns(origin)],
            back_send.at[g],
            back_relay_recv.at[g],
            lambda origin: back_recv.at[g, origin],
        )

    send_home(1)

    def query_step(n, carry):
        i, at, span = block_of(n)
        dq_out[i, at, :] = dot_nn(score_grad[i, at, :], window[0, span, :]).astype(BF16)
        return carry

    lax.fori_loop(0, 2 * blocks, query_step, 0)
    write_out(1, dq_out, dq_hbm)
    send_home(0)
    relay_home(1)
    relay_home(0)

    for copy in self_results:
        copy.wait()
    for g, target in ((1, dv_hbm), (0, dk_hbm)):
        for r in (3, 1, 2, 0):
            for source_core in range(2):
                origin = relative[r] * 2 + (1 - core if r == 3 else source_core)
                if r == 3 and source_core:
                    continue
                arrived(result.at[g, :, columns(origin)], back_recv.at[g, origin])
        copy = pltpu.make_async_copy(result.at[g], target, result_sem.at[g])
        copy.start()
        outs.append(copy)
    for copy, wanted in sends:
        if wanted is None:
            copy.wait_send()
        else:

            @pl.when(wanted)
            def _():
                copy.wait_send()

    for copy in outs:
        copy.wait()


def on_device(n_ctx, queries, keys, values, doc_ids, output_gradient):
    rows, width = queries.shape
    piece, key_width = keys.shape
    heads = width // HEAD_SIZE
    all_rows = (SPAN + 1) * rows
    stacked = heads * TILE
    reach = SPAN * rows + TILE
    docs = doc_ids.reshape(-1, TILE)
    vmem = pltpu.VMEM
    dma = pltpu.SemaphoreType.DMA
    any_space = pl.BlockSpec(memory_space=pl.ANY)
    return pl.pallas_call(
        functools.partial(kernel, n_ctx),
        out_shape=(
            jax.ShapeDtypeStruct((rows, width), BF16),
            jax.ShapeDtypeStruct((rows, width), BF16),
            jax.ShapeDtypeStruct((piece, key_width), BF16),
            jax.ShapeDtypeStruct((piece, key_width), BF16),
        ),
        in_specs=[any_space] * 5,
        out_specs=(any_space,) * 4,
        scratch_shapes=[
            vmem((2, piece, key_width), BF16),
            vmem((2, all_rows, HEAD_SIZE), BF16),
            vmem((2, 2, piece, HEAD_SIZE), BF16),
            vmem(docs.shape, jnp.int32),
            vmem((2, stacked, HEAD_SIZE), BF16),
            vmem((2, stacked, HEAD_SIZE), BF16),
            vmem((2, HEAD_SIZE, stacked), BF16),
            vmem((2, HEAD_SIZE, stacked), BF16),
            vmem((2, TILE, reach), F32),
            vmem((2, stacked, reach), F32),
            vmem((2, stacked, reach), BF16),
            vmem((2, stacked, reach), BF16),
            vmem((2, stacked, HEAD_SIZE), BF16),
            vmem((2, stacked, HEAD_SIZE), BF16),
            vmem((2, HEAD_SIZE, all_rows), F32),
            vmem((2, SPAN * rows, HEAD_SIZE), BF16),
            vmem((2, rows, HEAD_SIZE), F32),
            vmem((2, SPAN, rows, HEAD_SIZE), BF16),
            vmem((2, rows, HEAD_SIZE), BF16),
            vmem((2, 2, piece, HEAD_SIZE), BF16),
            vmem((2, piece, key_width), BF16),
            dma((3,)),
            dma((2, 2, heads)),
            dma((4,)),
            dma((2, 2, heads)),
            dma((2,)),
            dma((2, 9)),
            dma((2, 2 * GROUPS)),
            dma((2, 2)),
            dma((2, SPAN, GROUPS)),
            dma((2, SPAN, GROUPS)),
            dma((2, SPAN, GROUPS)),
            dma((2, SPAN, GROUPS)),
            dma((2, 9)),
            dma((2, 2 * GROUPS)),
            dma((2, 2)),
        ],
        compiler_params=pltpu.CompilerParams(collective_id=0, has_side_effects=True),
    )(queries, keys, values, docs, output_gradient)


def solution(mesh):
    in_specs = (
        P("ctx", "head"),
        P(("ctx", "head"), None),
        P(("ctx", "head"), None),
        P(),
        P("ctx", "head"),
    )
    out_specs = (
        P("ctx", "head"),
        P("ctx", "head"),
        P(("ctx", "head"), None),
        P(("ctx", "head"), None),
    )
    return jax.shard_map(
        functools.partial(on_device, mesh.shape["ctx"]),
        mesh=mesh,
        in_specs=in_specs,
        out_specs=out_specs,
        check_vma=False,
    )
```

```python
import functools
import math

import jax
import jax.numpy as jnp
from jax import lax
from jax.experimental import pallas as pl
from jax.experimental.pallas import tpu as pltpu
from jax.sharding import PartitionSpec as P

HEAD_SIZE = 128
TILE = 128
SPAN = 2
BLOCK_HEADS = 2
GROUPS = 4
SCALE = HEAD_SIZE ** -0.5
EXP2_SCALE = SCALE * math.log2(math.e)
MASKED = -1e30
LIMIT = 40 << 20
MESH = pl.DeviceIdType.MESH
F32 = jnp.float32
BF16 = jnp.bfloat16


def dot_nt(a, b):
    return lax.dot_general(a, b, (((1,), (1,)), ((), ())), preferred_element_type=F32)


def dot_nn(a, b):
    return lax.dot_general(a, b, (((1,), (0,)), ((), ())), preferred_element_type=F32)


def kernel(
    n_ctx,
    q_hbm,
    k_hbm,
    v_hbm,
    doc_hbm,
    g_hbm,
    att_out,
    dq_out,
    dk_out,
    dv_out,
    stage,
    window,
    relay,
    doc,
    qs,
    gs,
    qt,
    gt,
    bias,
    probs,
    weights,
    score_grad,
    held,
    row_held,
    acc,
    part,
    own,
    got,
    home,
    back_relay,
    result,
    load_sem,
    head_load_sem,
    self_sem,
    fwd_send,
    fwd_recv,
    fwd_relay_recv,
    ctx_send,
    ctx_recv,
    back_ctx_send,
    back_ctx_recv,
    back_send,
    back_recv,
    back_relay_recv,
):
    rows = TILE * 2
    piece = stage.shape[1]
    group_rows = 2 * piece
    heads = qs.shape[1] // TILE
    reach = SPAN * rows + TILE
    ctx = lax.axis_index("ctx")
    head = lax.axis_index("head")
    zone = head // 2
    core = lax.rem(head, 2)

    def zone_at(offset):
        return lax.rem(zone + offset, GROUPS)

    far, plus, minus = zone_at(2), zone_at(1), zone_at(3)
    relative = (far, plus, minus, zone)
    partner = zone * 2 + (1 - core)

    has_later = (ctx + 1 < n_ctx, ctx + 2 < n_ctx)
    has_earlier = (ctx >= 1, ctx >= 2)

    barrier = pltpu.get_barrier_semaphore()
    for peer in (plus * 2, plus * 2 + 1, minus * 2, minus * 2 + 1, partner):
        pl.semaphore_signal(barrier, inc=1, device_id=(ctx, peer), device_id_type=MESH)
    for dist in (1, 2):

        @pl.when(has_later[dist - 1])
        def _():
            pl.semaphore_signal(
                barrier, inc=1, device_id=(ctx + dist, head), device_id_type=MESH
            )

        @pl.when(has_earlier[dist - 1])
        def _():
            pl.semaphore_signal(
                barrier, inc=1, device_id=(ctx - dist, head), device_id_type=MESH
            )

    loads = [
        pltpu.make_async_copy(k_hbm, stage.at[0], load_sem.at[0]),
        pltpu.make_async_copy(v_hbm, stage.at[1], load_sem.at[1]),
        pltpu.make_async_copy(doc_hbm, doc, load_sem.at[2]),
    ]
    for copy in loads:
        copy.start()

    def columns(of_head):
        return pl.ds(pl.multiple_of(of_head * HEAD_SIZE, HEAD_SIZE), HEAD_SIZE)

    def piece_rows(of_head, base=0):
        return pl.ds(pl.multiple_of(base + of_head * piece, piece), piece)

    def zone_rows(of_zone, base=0):
        return pl.ds(pl.multiple_of(base + of_zone * group_rows, group_rows), group_rows)

    sends = []

    def remote(source, target, send_sem, recv_sem, device):
        return pltpu.make_async_remote_copy(
            src_ref=source,
            dst_ref=target,
            send_sem=send_sem,
            recv_sem=recv_sem,
            device_id=device,
            device_id_type=MESH,
        )

    def send(source, target, send_sem, recv_sem, device):
        copy = remote(source, target, send_sem, recv_sem, device)
        copy.start()
        sends.append((copy, None))

    def send_if(wanted, source, target, send_sem, recv_sem, device):
        copy = remote(source, target, send_sem, recv_sem, device)

        @pl.when(wanted)
        def _():
            copy.start()

        sends.append((copy, wanted))

    def arrived(target, recv_sem):
        remote(target, target, fwd_send.at[0, 0], recv_sem, (ctx, partner)).wait_recv()

    def exchange_far(source_of, relay_ref, send_sem, recv_sem):
        for way, (middle, target_core) in enumerate(((plus, core), (minus, 1 - core))):
            send(
                source_of(far * 2 + target_core),
                relay_ref.at[way],
                send_sem.at[way],
                recv_sem.at[way],
                (ctx, middle * 2 + target_core),
            )

    def exchange_near(source_of, target, zone_number, send_sem, recv_sem, slot):
        for target_core in range(2):
            peer = zone_number * 2 + target_core
            send(source_of(peer), target, send_sem.at[slot + target_core], recv_sem, (ctx, peer))

    def pass_on(relay_ref, target_of, send_sem, relay_recv, recv_of):
        for way, (after, origin) in enumerate(
            ((plus, minus * 2 + core), (minus, plus * 2 + (1 - core)))
        ):
            arrived(relay_ref.at[way], relay_recv.at[way])
            send(
                relay_ref.at[way],
                target_of(origin),
                send_sem.at[7 + way],
                recv_of(origin),
                (ctx, after * 2 + core),
            )

    def stage_of(a):
        return lambda to_head: stage.at[a, :, columns(to_head)]

    def mine_of(a):
        return window.at[a, piece_rows(head, SPAN * rows), :]

    def start_far(a):
        exchange_far(stage_of(a), relay.at[a], fwd_send.at[a], fwd_relay_recv.at[a])

    def start_partner(a):
        send(
            stage_of(a)(partner),
            mine_of(a),
            fwd_send.at[a, 6],
            fwd_recv.at[a, head],
            (ctx, partner),
        )

    def start_near(a):
        for zone_number, slot in ((plus, 2), (minus, 4)):
            exchange_near(
                stage_of(a),
                mine_of(a),
                zone_number,
                fwd_send.at[a],
                fwd_recv.at[a, head],
                slot,
            )

    def window_piece(a, of_head):
        return window.at[a, piece_rows(of_head, SPAN * rows), :]

    def hand_on(a, r):
        group = relative[r]
        if r == 3:
            self_copies[a].wait()
            arrived(window_piece(a, partner), fwd_recv.at[a, partner])
        else:
            for source_core in range(2):
                origin = group * 2 + source_core
                arrived(window_piece(a, origin), fwd_recv.at[a, origin])
        for dist in (1, 2):
            send_if(
                has_later[dist - 1],
                window.at[a, zone_rows(group, SPAN * rows), :],
                window.at[a, zone_rows(group, (SPAN - dist) * rows), :],
                ctx_send.at[a, dist - 1, r],
                ctx_recv.at[a, dist - 1, r],
                (ctx + dist, head),
            )

    def relay_forward(a):
        pass_on(
            relay.at[a],
            lambda origin: window_piece(a, origin),
            fwd_send.at[a],
            fwd_relay_recv.at[a],
            lambda origin: fwd_recv.at[a, origin],
        )

    loads[0].wait()
    loads[1].wait()
    self_copies = []
    for a in range(2):
        copy = pltpu.make_async_copy(
            stage.at[a, :, columns(head)],
            window.at[a, piece_rows(head, SPAN * rows), :],
            self_sem.at[a],
        )
        copy.start()
        self_copies.append(copy)

    pl.semaphore_wait(
        barrier,
        5
        + has_later[0].astype(jnp.int32)
        + has_later[1].astype(jnp.int32)
        + has_earlier[0].astype(jnp.int32)
        + has_earlier[1].astype(jnp.int32),
    )
    start_far(0)

    head_loads = []
    for which, (source, target) in enumerate(((q_hbm, qs), (g_hbm, gs))):
        for i in range(2):
            for h in range(heads):
                copy = pltpu.make_async_copy(
                    source.at[pl.ds(i * TILE, TILE), pl.ds(h * TILE, TILE)],
                    target.at[i, pl.ds(h * TILE, TILE), :],
                    head_load_sem.at[which, i, h],
                )
                copy.start()
                head_loads.append(copy)
    loads[2].wait()

    row_place = lax.broadcasted_iota(jnp.int32, (TILE, TILE), 0)
    column_place = lax.broadcasted_iota(jnp.int32, (TILE, TILE), 1)
    for i in range(2):
        query_docs = jnp.broadcast_to(
            doc[pl.ds(2 * ctx + i, 1), :].astype(F32), (TILE, TILE)
        ).T
        for j in range(5):
            doc_row = 2 * ctx - 2 * SPAN + i + j
            key_docs = doc[pl.ds(jnp.maximum(doc_row, 0), 1), :].astype(F32)
            seen = query_docs == key_docs
            if j == 4:
                seen = seen & (column_place <= row_place)
            outside = jnp.where(doc_row >= 0, 0.0, MASKED).astype(F32)
            bias[i, :, pl.ds(j * TILE, TILE)] = jnp.where(seen, 0.0, MASKED) + outside

    start_partner(0)
    start_near(0)
    start_partner(1)
    hand_on(0, 3)

    for copy in head_loads:
        copy.wait()
    for i in range(2):
        for h in range(heads):
            at = pl.ds(h * TILE, TILE)
            qt[i, :, at] = qs[i, at, :].T
            gt[i, :, at] = gs[i, at, :].T

    start_far(1)
    hand_on(1, 3)

    zero_block = jnp.zeros((rows, HEAD_SIZE), BF16)

    @pl.when(ctx < 1)
    def _():
        for a in range(2):
            window[a, pl.ds(rows, rows), :] = zero_block

    @pl.when(ctx < 2)
    def _():
        for a in range(2):
            window[a, pl.ds(0, rows), :] = zero_block

    for dist in (1, 2):

        @pl.when(ctx + dist >= n_ctx)
        def _():
            for a in range(2):
                got[a, dist - 1] = zero_block

    acc[...] = jnp.zeros_like(acc)

    relay_forward(0)
    start_near(1)
    hand_on(0, 1)
    hand_on(0, 2)
    relay_forward(1)
    hand_on(0, 0)

    def window_here(a):
        for r in (3, 1, 2, 0):
            for dist in (1, 2):

                @pl.when(has_earlier[dist - 1])
                def _():
                    arrived(
                        window.at[a, zone_rows(relative[r], (SPAN - dist) * rows), :],
                        ctx_recv.at[a, dist - 1, r],
                    )

    blocks = heads // BLOCK_HEADS
    block_rows = BLOCK_HEADS * TILE

    def block_of(n):
        i = n // blocks
        return i, pl.ds(n % blocks * block_rows, block_rows), pl.ds(i * TILE, reach)

    def put_heads(out, n, block):
        at_rows = pl.ds(n // blocks * TILE, TILE)
        first = n % blocks * BLOCK_HEADS
        for h in range(BLOCK_HEADS):
            at_columns = pl.ds((first + h) * HEAD_SIZE, HEAD_SIZE)
            out[at_rows, at_columns] = block[h * TILE : (h + 1) * TILE]

    hand_on(1, 1)
    hand_on(1, 2)
    window_here(0)
    hand_on(1, 0)

    every = reach // TILE

    def score_stage(n):
        i, at, span = block_of(n)
        mask = bias[i]
        scores = dot_nt(qs[i, at, :], window[0, span, :])
        scores = scores + jnp.concatenate([mask] * BLOCK_HEADS, 0)
        held[n % 2] = scores
        row_max = jnp.max(scores, axis=1, keepdims=True)
        row_held[n % 2] = jnp.broadcast_to(row_max, (block_rows, TILE))

    def probability_stage(n):
        i, at, span = block_of(n)
        row_max = jnp.concatenate([row_held[n % 2]] * every, 1)
        raised = jnp.exp2((held[n % 2] - row_max) * EXP2_SCALE)
        inverse = 1.0 / jnp.sum(raised, axis=1, keepdims=True)
        probability = raised * inverse
        probs[i, at, :] = probability
        weights[i, at, :] = probability.astype(BF16)

    score_stage(0)
    for n in range(2 * blocks):
        if n + 1 < 2 * blocks:
            score_stage(n + 1)
        probability_stage(n)

    def collect(g, left, right):
        for i in range(2):
            span = pl.ds(i * TILE, reach)
            acc[g, :, span] = acc[g, :, span] + dot_nn(left[i], right[i])
        for t in range(2 * SPAN + 2):
            block = acc[g, :, pl.ds(t * TILE, TILE)].T
            if t < 2 * SPAN:
                part[g, pl.ds(t * TILE, TILE), :] = block.astype(BF16)
            else:
                own[g, pl.ds(t * TILE - SPAN * rows, TILE), :] = block
        for r in range(GROUPS):
            for dist in (1, 2):
                send_if(
                    has_earlier[dist - 1],
                    part.at[g, zone_rows(relative[r], (SPAN - dist) * rows), :],
                    got.at[g, dist - 1, zone_rows(relative[r]), :],
                    back_ctx_send.at[g, dist - 1, r],
                    back_ctx_recv.at[g, dist - 1, r],
                    (ctx - dist, head),
                )

    collect(1, gt, weights)

    window_here(1)

    def output_stage(n):
        i, at, span = block_of(n)
        attended = dot_nn(weights[i, at, :], window[1, span, :]).astype(BF16)
        put_heads(att_out, n, attended)
        delta = jnp.sum(
            gs[i, at, :].astype(F32) * attended.astype(F32), axis=1, keepdims=True
        )
        row_held[n % 2] = jnp.broadcast_to(delta, (block_rows, TILE))

    def gradient_stage(n):
        i, at, span = block_of(n)
        prob_grad = dot_nt(gs[i, at, :], window[1, span, :])
        delta = jnp.concatenate([row_held[n % 2]] * every, 1)
        score_grad[i, at, :] = (probs[i, at, :] * (prob_grad - delta) * SCALE).astype(BF16)

    output_stage(0)
    for n in range(2 * blocks):
        if n + 1 < 2 * blocks:
            output_stage(n + 1)
        gradient_stage(n)

    collect(0, qt, score_grad)

    self_results = []

    def send_home(g):
        mine = result.at[g, :, columns(head)]
        source_of = lambda to_head: home.at[g, piece_rows(to_head), :]
        for r in range(GROUPS):
            at = zone_rows(relative[r])
            for dist in (1, 2):

                @pl.when(has_later[dist - 1])
                def _():
                    arrived(got.at[g, dist - 1, at, :], back_ctx_recv.at[g, dist - 1, r])

            total = own[g, at, :] + got[g, 0, at, :].astype(F32) + got[g, 1, at, :].astype(F32)
            home[g, at, :] = total.astype(BF16)
            if r == 0:
                exchange_far(source_of, back_relay.at[g], back_send.at[g], back_relay_recv.at[g])
            elif r < 3:
                exchange_near(
                    source_of, mine, relative[r], back_send.at[g], back_recv.at[g, head], 2 * r
                )
            else:
                send(
                    source_of(partner),
                    mine,
                    back_send.at[g, 6],
                    back_recv.at[g, head],
                    (ctx, partner),
                )
                copy = pltpu.make_async_copy(source_of(head), mine, self_sem.at[2 + g])
                copy.start()
                self_results.append(copy)

    def relay_home(g):
        pass_on(
            back_relay.at[g],
            lambda origin: result.at[g, :, columns(origin)],
            back_send.at[g],
            back_relay_recv.at[g],
            lambda origin: back_recv.at[g, origin],
        )

    send_home(1)

    for n in range(2 * blocks):
        i, at, span = block_of(n)
        put_heads(dq_out, n, dot_nn(score_grad[i, at, :], window[0, span, :]).astype(BF16))

    send_home(0)
    relay_home(1)
    relay_home(0)

    for copy in self_results:
        copy.wait()
    for g, target in ((1, dv_out), (0, dk_out)):
        for r in (3, 1, 2, 0):
            for source_core in range(2):
                origin = relative[r] * 2 + (1 - core if r == 3 else source_core)
                if r == 3 and source_core:
                    continue
                arrived(result.at[g, :, columns(origin)], back_recv.at[g, origin])
        target[...] = result[g]
    for copy, wanted in sends:
        if wanted is None:
            copy.wait_send()
        else:

            @pl.when(wanted)
            def _():
                copy.wait_send()


def on_device(n_ctx, queries, keys, values, doc_ids, output_gradient):
    rows, width = queries.shape
    piece, key_width = keys.shape
    heads = width // HEAD_SIZE
    all_rows = (SPAN + 1) * rows
    stacked = heads * TILE
    reach = SPAN * rows + TILE
    docs = doc_ids.reshape(-1, TILE)
    in_hbm = [
        pltpu.with_memory_space_constraint(x, pltpu.HBM)
        for x in (queries, keys, values, docs, output_gradient)
    ]
    vmem = pltpu.VMEM
    dma = pltpu.SemaphoreType.DMA
    any_space = pl.BlockSpec(memory_space=pl.ANY)
    results = pl.pallas_call(
        functools.partial(kernel, n_ctx),
        out_shape=(
            jax.ShapeDtypeStruct((rows, width), BF16),
            jax.ShapeDtypeStruct((rows, width), BF16),
            jax.ShapeDtypeStruct((piece, key_width), BF16),
            jax.ShapeDtypeStruct((piece, key_width), BF16),
        ),
        in_specs=[pl.BlockSpec(memory_space=pltpu.HBM)] * 5,
        out_specs=(pl.BlockSpec(memory_space=pltpu.VMEM),) * 4,
        scratch_shapes=[
            vmem((2, piece, key_width), BF16),
            vmem((2, all_rows, HEAD_SIZE), BF16),
            vmem((2, 2, piece, HEAD_SIZE), BF16),
            vmem(docs.shape, jnp.int32),
            vmem((2, stacked, HEAD_SIZE), BF16),
            vmem((2, stacked, HEAD_SIZE), BF16),
            vmem((2, HEAD_SIZE, stacked), BF16),
            vmem((2, HEAD_SIZE, stacked), BF16),
            vmem((2, TILE, reach), F32),
            vmem((2, stacked, reach), F32),
            vmem((2, stacked, reach), BF16),
            vmem((2, stacked, reach), BF16),
            vmem((2, BLOCK_HEADS * TILE, reach), F32),
            vmem((2, BLOCK_HEADS * TILE, TILE), F32),
            vmem((2, HEAD_SIZE, all_rows), F32),
            vmem((2, SPAN * rows, HEAD_SIZE), BF16),
            vmem((2, rows, HEAD_SIZE), F32),
            vmem((2, SPAN, rows, HEAD_SIZE), BF16),
            vmem((2, rows, HEAD_SIZE), BF16),
            vmem((2, 2, piece, HEAD_SIZE), BF16),
            vmem((2, piece, key_width), BF16),
            dma((3,)),
            dma((2, 2, heads)),
            dma((4,)),
            dma((2, 9)),
            dma((2, 2 * GROUPS)),
            dma((2, 2)),
            dma((2, SPAN, GROUPS)),
            dma((2, SPAN, GROUPS)),
            dma((2, SPAN, GROUPS)),
            dma((2, SPAN, GROUPS)),
            dma((2, 9)),
            dma((2, 2 * GROUPS)),
            dma((2, 2)),
        ],
        compiler_params=pltpu.CompilerParams(
            collective_id=0, has_side_effects=True, vmem_limit_bytes=LIMIT
        ),
    )(*in_hbm)
    return write_results(results)


def write_kernel(*refs):
    count = len(refs) // 2
    sources, targets, sem = refs[:count], refs[count : 2 * count], refs[-1]
    copies = [
        pltpu.make_async_copy(source, target, sem.at[n])
        for n, (source, target) in enumerate(zip(sources, targets))
    ]
    for copy in copies:
        copy.start()
    for copy in copies:
        copy.wait()


def write_results(results):
    return pl.pallas_call(
        write_kernel,
        out_shape=tuple(jax.ShapeDtypeStruct(r.shape, r.dtype) for r in results),
        in_specs=[pl.BlockSpec(memory_space=pltpu.VMEM)] * len(results),
        out_specs=(pl.BlockSpec(memory_space=pl.ANY),) * len(results),
        scratch_shapes=[pltpu.SemaphoreType.DMA((len(results),))],
        compiler_params=pltpu.CompilerParams(vmem_limit_bytes=LIMIT),
    )(*results)


def solution(mesh):
    in_specs = (
        P("ctx", "head"),
        P(("ctx", "head"), None),
        P(("ctx", "head"), None),
        P(),
        P("ctx", "head"),
    )
    out_specs = (
        P("ctx", "head"),
        P("ctx", "head"),
        P(("ctx", "head"), None),
        P(("ctx", "head"), None),
    )
    return jax.shard_map(
        functools.partial(on_device, mesh.shape["ctx"]),
        mesh=mesh,
        in_specs=in_specs,
        out_specs=out_specs,
        check_vma=False,
    )
```

```python
import functools
import math

import jax
import jax.numpy as jnp
from jax import lax
from jax.experimental import pallas as pl
from jax.experimental.pallas import tpu as pltpu
from jax.sharding import PartitionSpec as P

HEAD_SIZE = 128
TILE = 128
SPAN = 2
BLOCK_HEADS = 2
GROUPS = 4
SCALE = HEAD_SIZE ** -0.5
EXP2_SCALE = SCALE * math.log2(math.e)
MASKED = -1e30
LIMIT = 40 << 20
MESH = pl.DeviceIdType.MESH
F32 = jnp.float32
BF16 = jnp.bfloat16


def dot_nt(a, b):
    return lax.dot_general(a, b, (((1,), (1,)), ((), ())), preferred_element_type=F32)


def dot_nn(a, b):
    return lax.dot_general(a, b, (((1,), (0,)), ((), ())), preferred_element_type=F32)


def kernel(
    n_ctx,
    q_hbm,
    k_hbm,
    v_hbm,
    doc_hbm,
    g_hbm,
    att_out,
    dq_out,
    dk_out,
    dv_out,
    stage,
    window,
    relay,
    doc,
    qs,
    gs,
    qt,
    gt,
    bias,
    probs,
    weights,
    score_grad,
    held,
    row_held,
    acc,
    part,
    own,
    got,
    home,
    back_relay,
    result,
    load_sem,
    head_load_sem,
    self_sem,
    fwd_send,
    fwd_recv,
    fwd_relay_recv,
    ctx_send,
    ctx_recv,
    back_ctx_send,
    back_ctx_recv,
    back_send,
    back_recv,
    back_relay_recv,
):
    rows = TILE * 2
    piece = stage.shape[1]
    group_rows = 2 * piece
    heads = qs.shape[1] // TILE
    reach = SPAN * rows + TILE
    ctx = lax.axis_index("ctx")
    head = lax.axis_index("head")
    zone = head // 2
    core = lax.rem(head, 2)

    def zone_at(offset):
        return lax.rem(zone + offset, GROUPS)

    far, plus, minus = zone_at(2), zone_at(1), zone_at(3)
    relative = (far, plus, minus, zone)
    partner = zone * 2 + (1 - core)

    has_later = (ctx + 1 < n_ctx, ctx + 2 < n_ctx)
    has_earlier = (ctx >= 1, ctx >= 2)

    barrier = pltpu.get_barrier_semaphore()
    for peer in (plus * 2, plus * 2 + 1, minus * 2, minus * 2 + 1, partner):
        pl.semaphore_signal(barrier, inc=1, device_id=(ctx, peer), device_id_type=MESH)
    for dist in (1, 2):

        @pl.when(has_later[dist - 1])
        def _():
            pl.semaphore_signal(
                barrier, inc=1, device_id=(ctx + dist, head), device_id_type=MESH
            )

        @pl.when(has_earlier[dist - 1])
        def _():
            pl.semaphore_signal(
                barrier, inc=1, device_id=(ctx - dist, head), device_id_type=MESH
            )

    loads = [
        pltpu.make_async_copy(k_hbm, stage.at[0], load_sem.at[0]),
        pltpu.make_async_copy(v_hbm, stage.at[1], load_sem.at[1]),
        pltpu.make_async_copy(doc_hbm, doc, load_sem.at[2]),
    ]
    for copy in loads:
        copy.start()

    def columns(of_head):
        return pl.ds(pl.multiple_of(of_head * HEAD_SIZE, HEAD_SIZE), HEAD_SIZE)

    def piece_rows(of_head, base=0):
        return pl.ds(pl.multiple_of(base + of_head * piece, piece), piece)

    def zone_rows(of_zone, base=0):
        return pl.ds(pl.multiple_of(base + of_zone * group_rows, group_rows), group_rows)

    sends = []

    def remote(source, target, send_sem, recv_sem, device):
        return pltpu.make_async_remote_copy(
            src_ref=source,
            dst_ref=target,
            send_sem=send_sem,
            recv_sem=recv_sem,
            device_id=device,
            device_id_type=MESH,
        )

    def send(source, target, send_sem, recv_sem, device):
        copy = remote(source, target, send_sem, recv_sem, device)
        copy.start()
        sends.append((copy, None))

    def send_if(wanted, source, target, send_sem, recv_sem, device):
        copy = remote(source, target, send_sem, recv_sem, device)

        @pl.when(wanted)
        def _():
            copy.start()

        sends.append((copy, wanted))

    def arrived(target, recv_sem):
        remote(target, target, fwd_send.at[0, 0], recv_sem, (ctx, partner)).wait_recv()

    def exchange_far(source_of, relay_ref, send_sem, recv_sem):
        for way, (middle, target_core) in enumerate(((plus, core), (minus, 1 - core))):
            send(
                source_of(far * 2 + target_core),
                relay_ref.at[way],
                send_sem.at[way],
                recv_sem.at[way],
                (ctx, middle * 2 + target_core),
            )

    def exchange_near(source_of, target, zone_number, send_sem, recv_sem, slot):
        for target_core in range(2):
            peer = zone_number * 2 + target_core
            send(source_of(peer), target, send_sem.at[slot + target_core], recv_sem, (ctx, peer))

    def pass_on(relay_ref, target_of, send_sem, relay_recv, recv_of):
        for way, (after, origin) in enumerate(
            ((plus, minus * 2 + core), (minus, plus * 2 + (1 - core)))
        ):
            arrived(relay_ref.at[way], relay_recv.at[way])
            send(
                relay_ref.at[way],
                target_of(origin),
                send_sem.at[7 + way],
                recv_of(origin),
                (ctx, after * 2 + core),
            )

    def stage_of(a):
        return lambda to_head: stage.at[a, :, columns(to_head)]

    def mine_of(a):
        return window.at[a, piece_rows(head, SPAN * rows), :]

    def start_far(a):
        exchange_far(stage_of(a), relay.at[a], fwd_send.at[a], fwd_relay_recv.at[a])

    def start_partner(a):
        send(
            stage_of(a)(partner),
            mine_of(a),
            fwd_send.at[a, 6],
            fwd_recv.at[a, head],
            (ctx, partner),
        )

    def start_near(a):
        for zone_number, slot in ((plus, 2), (minus, 4)):
            exchange_near(
                stage_of(a),
                mine_of(a),
                zone_number,
                fwd_send.at[a],
                fwd_recv.at[a, head],
                slot,
            )

    def window_piece(a, of_head):
        return window.at[a, piece_rows(of_head, SPAN * rows), :]

    def hand_on(a, r):
        group = relative[r]
        if r == 3:
            self_copies[a].wait()
            arrived(window_piece(a, partner), fwd_recv.at[a, partner])
        else:
            for source_core in range(2):
                origin = group * 2 + source_core
                arrived(window_piece(a, origin), fwd_recv.at[a, origin])
        for dist in (1, 2):
            send_if(
                has_later[dist - 1],
                window.at[a, zone_rows(group, SPAN * rows), :],
                window.at[a, zone_rows(group, (SPAN - dist) * rows), :],
                ctx_send.at[a, dist - 1, r],
                ctx_recv.at[a, dist - 1, r],
                (ctx + dist, head),
            )

    def relay_forward(a):
        pass_on(
            relay.at[a],
            lambda origin: window_piece(a, origin),
            fwd_send.at[a],
            fwd_relay_recv.at[a],
            lambda origin: fwd_recv.at[a, origin],
        )

    loads[0].wait()
    loads[1].wait()
    self_copies = []
    for a in range(2):
        copy = pltpu.make_async_copy(
            stage.at[a, :, columns(head)],
            window.at[a, piece_rows(head, SPAN * rows), :],
            self_sem.at[a],
        )
        copy.start()
        self_copies.append(copy)

    pl.semaphore_wait(
        barrier,
        5
        + has_later[0].astype(jnp.int32)
        + has_later[1].astype(jnp.int32)
        + has_earlier[0].astype(jnp.int32)
        + has_earlier[1].astype(jnp.int32),
    )
    start_far(0)

    head_loads = []
    for which, (source, target) in enumerate(((q_hbm, qs), (g_hbm, gs))):
        for i in range(2):
            for h in range(heads):
                copy = pltpu.make_async_copy(
                    source.at[pl.ds(i * TILE, TILE), pl.ds(h * TILE, TILE)],
                    target.at[i, pl.ds(h * TILE, TILE), :],
                    head_load_sem.at[which, i, h],
                )
                copy.start()
                head_loads.append(copy)
    loads[2].wait()

    row_place = lax.broadcasted_iota(jnp.int32, (TILE, TILE), 0)
    column_place = lax.broadcasted_iota(jnp.int32, (TILE, TILE), 1)
    for i in range(2):
        query_docs = jnp.broadcast_to(
            doc[pl.ds(2 * ctx + i, 1), :].astype(F32), (TILE, TILE)
        ).T
        for j in range(5):
            doc_row = 2 * ctx - 2 * SPAN + i + j
            key_docs = doc[pl.ds(jnp.maximum(doc_row, 0), 1), :].astype(F32)
            seen = query_docs == key_docs
            if j == 4:
                seen = seen & (column_place <= row_place)
            outside = jnp.where(doc_row >= 0, 0.0, MASKED).astype(F32)
            bias[i, :, pl.ds(j * TILE, TILE)] = jnp.where(seen, 0.0, MASKED) + outside

    start_partner(0)
    start_near(0)
    start_partner(1)
    hand_on(0, 3)

    for copy in head_loads:
        copy.wait()
    for i in range(2):
        for h in range(heads):
            at = pl.ds(h * TILE, TILE)
            qt[i, :, at] = qs[i, at, :].T
            gt[i, :, at] = gs[i, at, :].T

    start_far(1)
    hand_on(1, 3)

    zero_block = jnp.zeros((rows, HEAD_SIZE), BF16)

    @pl.when(ctx < 1)
    def _():
        for a in range(2):
            window[a, pl.ds(rows, rows), :] = zero_block

    @pl.when(ctx < 2)
    def _():
        for a in range(2):
            window[a, pl.ds(0, rows), :] = zero_block

    for dist in (1, 2):

        @pl.when(ctx + dist >= n_ctx)
        def _():
            for a in range(2):
                got[a, dist - 1] = zero_block

    acc[...] = jnp.zeros_like(acc)

    relay_forward(0)
    start_near(1)
    hand_on(0, 1)
    hand_on(0, 2)
    relay_forward(1)
    hand_on(0, 0)

    def window_here(a):
        for r in (3, 1, 2, 0):
            for dist in (1, 2):

                @pl.when(has_earlier[dist - 1])
                def _():
                    arrived(
                        window.at[a, zone_rows(relative[r], (SPAN - dist) * rows), :],
                        ctx_recv.at[a, dist - 1, r],
                    )

    blocks = heads // BLOCK_HEADS
    block_rows = BLOCK_HEADS * TILE

    def block_of(n):
        i = n // blocks
        return i, pl.ds(n % blocks * block_rows, block_rows), pl.ds(i * TILE, reach)

    def put_heads(out, n, block):
        at_rows = pl.ds(n // blocks * TILE, TILE)
        first = n % blocks * BLOCK_HEADS
        for h in range(BLOCK_HEADS):
            at_columns = pl.ds((first + h) * HEAD_SIZE, HEAD_SIZE)
            out[at_rows, at_columns] = block[h * TILE : (h + 1) * TILE]

    hand_on(1, 1)
    hand_on(1, 2)
    window_here(0)
    hand_on(1, 0)

    every = reach // TILE

    def score_stage(n):
        i, at, span = block_of(n)
        mask = bias[i]
        scores = dot_nt(qs[i, at, :], window[0, span, :])
        scores = scores + jnp.concatenate([mask] * BLOCK_HEADS, 0)
        held[n % 2] = scores
        row_max = jnp.max(scores, axis=1, keepdims=True)
        row_held[n % 2] = jnp.broadcast_to(row_max, (block_rows, TILE))

    def probability_stage(n):
        i, at, span = block_of(n)
        row_max = jnp.concatenate([row_held[n % 2]] * every, 1)
        raised = jnp.exp2((held[n % 2] - row_max) * EXP2_SCALE)
        inverse = 1.0 / jnp.sum(raised, axis=1, keepdims=True)
        probability = raised * inverse
        probs[i, at, :] = probability
        weights[i, at, :] = probability.astype(BF16)

    score_stage(0)
    for n in range(2 * blocks):
        if n + 1 < 2 * blocks:
            score_stage(n + 1)
        probability_stage(n)

    def collect(g, left, right):
        for i in range(2):
            span = pl.ds(i * TILE, reach)
            acc[g, :, span] = acc[g, :, span] + dot_nn(left[i], right[i])
        for t in range(2 * SPAN + 2):
            block = acc[g, :, pl.ds(t * TILE, TILE)].T
            if t < 2 * SPAN:
                part[g, pl.ds(t * TILE, TILE), :] = block.astype(BF16)
            else:
                own[g, pl.ds(t * TILE - SPAN * rows, TILE), :] = block
        for r in range(GROUPS):
            for dist in (1, 2):
                send_if(
                    has_earlier[dist - 1],
                    part.at[g, zone_rows(relative[r], (SPAN - dist) * rows), :],
                    got.at[g, dist - 1, zone_rows(relative[r]), :],
                    back_ctx_send.at[g, dist - 1, r],
                    back_ctx_recv.at[g, dist - 1, r],
                    (ctx - dist, head),
                )

    collect(1, gt, weights)

    window_here(1)

    def output_stage(n):
        i, at, span = block_of(n)
        attended = dot_nn(weights[i, at, :], window[1, span, :]).astype(BF16)
        put_heads(att_out, n, attended)
        delta = jnp.sum(
            gs[i, at, :].astype(F32) * attended.astype(F32), axis=1, keepdims=True
        )
        row_held[n % 2] = jnp.broadcast_to(delta, (block_rows, TILE))

    def gradient_stage(n):
        i, at, span = block_of(n)
        prob_grad = dot_nt(gs[i, at, :], window[1, span, :])
        delta = jnp.concatenate([row_held[n % 2]] * every, 1)
        score_grad[i, at, :] = (probs[i, at, :] * (prob_grad - delta) * SCALE).astype(BF16)

    output_stage(0)
    for n in range(2 * blocks):
        if n + 1 < 2 * blocks:
            output_stage(n + 1)
        gradient_stage(n)

    collect(0, qt, score_grad)

    self_results = []

    def send_home(g, zones):
        mine = result.at[g, :, columns(head)]
        source_of = lambda to_head: home.at[g, piece_rows(to_head), :]
        for r in zones:
            at = zone_rows(relative[r])
            for dist in (1, 2):

                @pl.when(has_later[dist - 1])
                def _():
                    arrived(got.at[g, dist - 1, at, :], back_ctx_recv.at[g, dist - 1, r])

            total = own[g, at, :] + got[g, 0, at, :].astype(F32) + got[g, 1, at, :].astype(F32)
            home[g, at, :] = total.astype(BF16)
            if r == 0:
                exchange_far(source_of, back_relay.at[g], back_send.at[g], back_relay_recv.at[g])
            elif r < 3:
                exchange_near(
                    source_of, mine, relative[r], back_send.at[g], back_recv.at[g, head], 2 * r
                )
            else:
                send(
                    source_of(partner),
                    mine,
                    back_send.at[g, 6],
                    back_recv.at[g, head],
                    (ctx, partner),
                )
                copy = pltpu.make_async_copy(source_of(head), mine, self_sem.at[2 + g])
                copy.start()
                self_results.append(copy)

    def relay_home(g):
        pass_on(
            back_relay.at[g],
            lambda origin: result.at[g, :, columns(origin)],
            back_send.at[g],
            back_relay_recv.at[g],
            lambda origin: back_recv.at[g, origin],
        )

    send_home(1, (0,))

    for n in range(2 * blocks):
        i, at, span = block_of(n)
        put_heads(dq_out, n, dot_nn(score_grad[i, at, :], window[0, span, :]).astype(BF16))

    send_home(0, (0,))
    send_home(1, (1, 2, 3))
    send_home(0, (1, 2, 3))
    relay_home(1)
    relay_home(0)

    for copy in self_results:
        copy.wait()
    for g, target in ((1, dv_out), (0, dk_out)):
        for r in (3, 1, 2, 0):
            for source_core in range(2):
                origin = relative[r] * 2 + (1 - core if r == 3 else source_core)
                if r == 3 and source_core:
                    continue
                arrived(result.at[g, :, columns(origin)], back_recv.at[g, origin])
        target[...] = result[g]
    for copy, wanted in sends:
        if wanted is None:
            copy.wait_send()
        else:

            @pl.when(wanted)
            def _():
                copy.wait_send()


def on_device(n_ctx, queries, keys, values, doc_ids, output_gradient):
    rows, width = queries.shape
    piece, key_width = keys.shape
    heads = width // HEAD_SIZE
    all_rows = (SPAN + 1) * rows
    stacked = heads * TILE
    reach = SPAN * rows + TILE
    docs = doc_ids.reshape(-1, TILE)
    in_hbm = [
        pltpu.with_memory_space_constraint(x, pltpu.HBM)
        for x in (queries, keys, values, docs, output_gradient)
    ]
    vmem = pltpu.VMEM
    dma = pltpu.SemaphoreType.DMA
    any_space = pl.BlockSpec(memory_space=pl.ANY)
    results = pl.pallas_call(
        functools.partial(kernel, n_ctx),
        out_shape=(
            jax.ShapeDtypeStruct((rows, width), BF16),
            jax.ShapeDtypeStruct((rows, width), BF16),
            jax.ShapeDtypeStruct((piece, key_width), BF16),
            jax.ShapeDtypeStruct((piece, key_width), BF16),
        ),
        in_specs=[pl.BlockSpec(memory_space=pltpu.HBM)] * 5,
        out_specs=(pl.BlockSpec(memory_space=pltpu.VMEM),) * 4,
        scratch_shapes=[
            vmem((2, piece, key_width), BF16),
            vmem((2, all_rows, HEAD_SIZE), BF16),
            vmem((2, 2, piece, HEAD_SIZE), BF16),
            vmem(docs.shape, jnp.int32),
            vmem((2, stacked, HEAD_SIZE), BF16),
            vmem((2, stacked, HEAD_SIZE), BF16),
            vmem((2, HEAD_SIZE, stacked), BF16),
            vmem((2, HEAD_SIZE, stacked), BF16),
            vmem((2, TILE, reach), F32),
            vmem((2, stacked, reach), F32),
            vmem((2, stacked, reach), BF16),
            vmem((2, stacked, reach), BF16),
            vmem((2, BLOCK_HEADS * TILE, reach), F32),
            vmem((2, BLOCK_HEADS * TILE, TILE), F32),
            vmem((2, HEAD_SIZE, all_rows), F32),
            vmem((2, SPAN * rows, HEAD_SIZE), BF16),
            vmem((2, rows, HEAD_SIZE), F32),
            vmem((2, SPAN, rows, HEAD_SIZE), BF16),
            vmem((2, rows, HEAD_SIZE), BF16),
            vmem((2, 2, piece, HEAD_SIZE), BF16),
            vmem((2, piece, key_width), BF16),
            dma((3,)),
            dma((2, 2, heads)),
            dma((4,)),
            dma((2, 9)),
            dma((2, 2 * GROUPS)),
            dma((2, 2)),
            dma((2, SPAN, GROUPS)),
            dma((2, SPAN, GROUPS)),
            dma((2, SPAN, GROUPS)),
            dma((2, SPAN, GROUPS)),
            dma((2, 9)),
            dma((2, 2 * GROUPS)),
            dma((2, 2)),
        ],
        compiler_params=pltpu.CompilerParams(
            collective_id=0, has_side_effects=True, vmem_limit_bytes=LIMIT
        ),
    )(*in_hbm)
    return write_results(results)


def write_kernel(*refs):
    count = len(refs) // 2
    sources, targets, sem = refs[:count], refs[count : 2 * count], refs[-1]
    copies = [
        pltpu.make_async_copy(source, target, sem.at[n])
        for n, (source, target) in enumerate(zip(sources, targets))
    ]
    for copy in copies:
        copy.start()
    for copy in copies:
        copy.wait()


def write_results(results):
    return pl.pallas_call(
        write_kernel,
        out_shape=tuple(jax.ShapeDtypeStruct(r.shape, r.dtype) for r in results),
        in_specs=[pl.BlockSpec(memory_space=pltpu.VMEM)] * len(results),
        out_specs=(pl.BlockSpec(memory_space=pl.ANY),) * len(results),
        scratch_shapes=[pltpu.SemaphoreType.DMA((len(results),))],
        compiler_params=pltpu.CompilerParams(vmem_limit_bytes=LIMIT),
    )(*results)


def solution(mesh):
    in_specs = (
        P("ctx", "head"),
        P(("ctx", "head"), None),
        P(("ctx", "head"), None),
        P(),
        P("ctx", "head"),
    )
    out_specs = (
        P("ctx", "head"),
        P("ctx", "head"),
        P(("ctx", "head"), None),
        P(("ctx", "head"), None),
    )
    return jax.shard_map(
        functools.partial(on_device, mesh.shape["ctx"]),
        mesh=mesh,
        in_specs=in_specs,
        out_specs=out_specs,
        check_vma=False,
    )
```
